32 devices in a mesh: ctx: 4 (over y, x), fsdp: 8 (over z, core).
Axes of the slice: x: 2, y: 2, z: 4, core: 2. Of those that a mesh axis runs over, the one named last changes fastest.
Arguments:
- layer_input: bfloat16 [8, 512, 4096], P('fsdp', 'ctx'), may hold values from -6 to 6
- xbc_raw: bfloat16 [8, 512, 6144], P('fsdp', 'ctx'), may hold values from -6 to 6
- dt_raw: bfloat16 [8, 512, 64], P('fsdp', 'ctx'), may hold values from -1.5 to 5.5
- grad_out: bfloat16 [8, 512, 4096], P('fsdp', 'ctx'), may hold values from -6 to 6
- w_xbc: bfloat16 [4096, 6144], P('fsdp', 'ctx'), may hold values from -0.09375 to 0.09375
- w_dt: bfloat16 [4096, 64], P('fsdp', 'ctx'), may hold values from -0.09375 to 0.09375
- conv_weight: float32 [4, 6144], P(None, 'ctx'), may hold values from -3 to 3
- dt_bias: float32 [64], P('ctx'), may hold values from -4 to -2
- decay_rate: float32 [64], P('ctx'), may hold values from 0.0009765625 to 0.6, as said below
- skip_gain: float32 [64], P('ctx'), may hold values from 0.5 to 1.5
Outputs:
- input_grad: bfloat16 [8, 512, 4096], P('fsdp', 'ctx')
- w_xbc_grad: bfloat16 [4096, 6144], P('fsdp', 'ctx')
- w_dt_grad: bfloat16 [4096, 64], P('fsdp', 'ctx')
- conv_grad: float32 [4, 6144], P(None, 'ctx')
- bias_grad: float32 [64], P('ctx')
- rate_grad: float32 [64], P('ctx')
- skip_grad: float32 [64], P('ctx')
The draws below stay inside these ranges and needn't reach their ends.
Inputs may be any that keep to these rules, and one draw needn't show every extreme that they name: `decay_rate`: positive decay rates.
All inputs are finite; a program needn't handle non-finite values.
Results may differ from the reference program's by a relative error of at most 0.019.
Values may be sent and summed in bfloat16 or wider, within the bound.
A program may use at most 128 MiB of HBM per device.

```python
import math
import jax
import jax.numpy as jnp
from jax import lax

D = 4096
HEADS = 64
HEAD_DIM = 64
STATE = 128
KCONV = 4
BLOCK = 128
HG = 8
CH = 6144
LEN = 512
SEQS = 8
N_CTX = 4


def draw_dt_raw(key, part):
    base_key, where_key, size_key = jax.random.split(key, 3)
    full_shape = (SEQS, LEN, HEADS)
    baseline = 0.5 * jnp.clip(jax.random.normal(base_key, full_shape, jnp.float32), -3.0, 3.0)
    bursty = (jax.random.uniform(where_key, (SEQS, LEN, 1), jnp.float32) < 3.0 / LEN).astype(jnp.float32)
    height = jax.random.uniform(size_key, (SEQS, LEN, 1), jnp.float32, 2.0, 4.0)
    return (baseline + bursty * height).astype(jnp.bfloat16)


def draw_decay_rate(key, part):
    low_log = math.log(1.0 / LEN)
    high_log = math.log(0.6)
    return jnp.exp(jax.random.uniform(key, (HEADS,), jnp.float32, low_log, high_log))


def block_levels(key, shape, cuts, least, high):
    loudness, own = 1.0, jax.random.fold_in(key, 6)
    for dim, shards_of in cuts:
        heights = jnp.exp(jax.random.uniform(jax.random.fold_in(own, dim), (shards_of,), jnp.float32, least / len(cuts), high / len(cuts)))
        loudness = loudness * jnp.repeat(heights, shape[dim] // shards_of).reshape([-1 if axis == dim else 1 for axis in range(len(shape))])
    return loudness


def scatter_about(key, dims, scale, limit, cuts=(), kind=jnp.bfloat16):
    values = scale * jax.random.normal(key, dims, jnp.float32)
    if cuts:
        values = values * block_levels(key, dims, cuts, -0.22, 0.18)
    return jnp.clip(values, -limit, limit).astype(kind)


def setup_inputs(seed: int = 0) -> dict:
    splits = jax.random.split(jax.random.key(seed), 11)
    layer_input = scatter_about(splits[0], (SEQS, LEN, D), 1.0, 6.0, ((0, 8), (1, 4)))
    xbc_raw = scatter_about(splits[1], (SEQS, LEN, CH), 1.0, 6.0, ((0, 8), (1, 4)))
    dt_raw = draw_dt_raw(jax.random.fold_in(splits[10], 71), 0)
    grad_out = scatter_about(splits[3], (SEQS, LEN, HEADS * HEAD_DIM), 1.0, 6.0, ((0, 8), (1, 4)))
    w_xbc = scatter_about(splits[4], (D, CH), D ** -0.5, 0.09375, ((0, 8), (1, 4)))
    w_dt = scatter_about(splits[5], (D, HEADS), D ** -0.5, 0.09375, ((0, 8), (1, 4)))
    conv_weight = scatter_about(splits[6], (KCONV, CH), 0.5, 3.0, ((1, 4),), jnp.float32)
    dt_bias = jnp.clip(-4.0 + 2.0 * jax.random.uniform(splits[7], (HEADS,), jnp.float32) ** block_levels(splits[7], (HEADS,), ((0, 4),), -0.2, 0.2), -4.0, -2.0)
    decay_rate = draw_decay_rate(jax.random.fold_in(splits[10], 71), 0)
    skip_gain = jnp.clip(0.5 + 1.0 * jax.random.uniform(splits[9], (HEADS,), jnp.float32) ** block_levels(splits[9], (HEADS,), ((0, 4),), -0.2, 0.2), 0.5, 1.5)
    return dict(layer_input=layer_input, xbc_raw=xbc_raw, dt_raw=dt_raw, grad_out=grad_out, w_xbc=w_xbc, w_dt=w_dt, conv_weight=conv_weight, dt_bias=dt_bias, decay_rate=decay_rate, skip_gain=skip_gain)


def block_scan(values, step_dt, decay, in_proj, out_proj):
    seq_len = values.shape[0]
    group_count = values.shape[1]
    block_count = seq_len // BLOCK
    blocked = values.reshape(block_count, BLOCK, group_count, HG, HEAD_DIM)
    step_blocks = step_dt.reshape(block_count, BLOCK, group_count, HG)
    keys_in = in_proj.reshape(block_count, BLOCK, group_count, STATE)
    keys_out = out_proj.reshape(block_count, BLOCK, group_count, STATE)
    cumulative = jnp.cumsum(step_blocks * decay, axis=1)
    row_index = lax.broadcasted_iota(jnp.int32, (BLOCK, BLOCK), 0)
    col_index = lax.broadcasted_iota(jnp.int32, (BLOCK, BLOCK), 1)
    causal = (row_index >= col_index)[None, :, :, None, None]
    gap_log = cumulative[:, :, None] - cumulative[:, None, :]
    falloff = jnp.where(causal, jnp.exp(jnp.where(causal, gap_log, 0.0)), 0.0)
    scores = jnp.einsum('nigs,njgs->nijg', keys_out, keys_in, preferred_element_type=jnp.float32)
    mixing = (scores[..., None] * falloff * step_blocks[:, None]).astype(jnp.bfloat16)
    within = jnp.einsum('nijgh,njghp->nighp', mixing, blocked, preferred_element_type=jnp.float32)
    to_end = jnp.exp(cumulative[:, -1:] - cumulative) * step_blocks
    weighted = (to_end[..., None] * blocked).astype(jnp.bfloat16)
    contrib = jnp.einsum('njghp,njgs->nghps', weighted, keys_in, preferred_element_type=jnp.float32)
    factors = jnp.exp(cumulative[:, -1])

    def advance(carried, inputs):
        factor, added = inputs
        return (factor[..., None, None] * carried + added, carried)
    start_state = jnp.zeros((group_count, HG, HEAD_DIM, STATE), jnp.float32)
    _, entering = lax.scan(advance, start_state, (factors, contrib))
    from_state = jnp.einsum('nigs,nghps->nighp', keys_out, entering.astype(jnp.bfloat16), preferred_element_type=jnp.float32)
    from_state = from_state * jnp.exp(cumulative)[..., None]
    return (within + from_state).reshape(seq_len, group_count, HG, HEAD_DIM)

def mixer_forward(raw_proj, dt_offsets, conv_weight, dt_bias, decay_rate, skip_gain):
    seq_len = raw_proj.shape[0]
    kernel_taps = conv_weight.shape[0]
    group_count = dt_bias.shape[0] // HG
    padded = jnp.pad(raw_proj.astype(jnp.float32), ((kernel_taps - 1, 0), (0, 0)))
    convolved = conv_weight[0] * padded[0:seq_len]
    for tap_index in range(1, kernel_taps):
        convolved = convolved + conv_weight[tap_index] * padded[tap_index:tap_index + seq_len]
    activated = (convolved * jax.nn.sigmoid(convolved)).astype(jnp.bfloat16)
    grouped = activated.reshape(seq_len, group_count, HG * HEAD_DIM + 2 * STATE)
    values = grouped[:, :, :HG * HEAD_DIM].reshape(seq_len, group_count, HG, HEAD_DIM)
    in_proj = grouped[:, :, HG * HEAD_DIM:HG * HEAD_DIM + STATE]
    out_proj = grouped[:, :, HG * HEAD_DIM + STATE:]
    step_dt = jax.nn.softplus(dt_offsets.astype(jnp.float32) + dt_bias).reshape(seq_len, group_count, HG)
    decay = -decay_rate.reshape(group_count, HG)
    scanned = block_scan(values, step_dt, decay, in_proj, out_proj)
    skipped = skip_gain.reshape(group_count, HG)[..., None] * values.astype(jnp.float32)
    return (scanned + skipped).reshape(seq_len, group_count * HG * HEAD_DIM)

def reference(layer_input, xbc_raw, dt_raw, grad_out, w_xbc, w_dt, conv_weight, dt_bias, decay_rate, skip_gain):
    grad_scale = 1.0 / math.sqrt(SEQS * LEN)
    block_cols = CH // N_CTX
    block_heads = HEADS // N_CTX

    def per_sequence(carry, inputs):
        tokens_in, raw_proj, dt_offsets, out_grad = inputs
        _, pullback = jax.vjp(mixer_forward, raw_proj, dt_offsets, conv_weight, dt_bias, decay_rate, skip_gain)
        d_raw, d_offsets, d_conv, d_bias, d_rate, d_skip = pullback(out_grad.astype(jnp.float32))
        input_grad = jnp.zeros((LEN, D), jnp.float32)
        for column_block in range(N_CTX):
            col_lo = column_block * block_cols
            head_lo = column_block * block_heads
            partial_term = jnp.dot(d_raw[:, col_lo:col_lo + block_cols], w_xbc[:, col_lo:col_lo + block_cols].T, preferred_element_type=jnp.float32)
            partial_term = partial_term + jnp.dot(d_offsets[:, head_lo:head_lo + block_heads], w_dt[:, head_lo:head_lo + block_heads].T, preferred_element_type=jnp.float32)
            input_grad = input_grad + partial_term.astype(jnp.bfloat16).astype(jnp.float32)
        grads_cat = jnp.concatenate([d_raw, d_offsets], axis=1)
        weight_term = jnp.dot(tokens_in.T, grads_cat, preferred_element_type=jnp.float32) * grad_scale
        weight_sum, conv_sum, bias_sum, rate_sum, skip_sum = carry
        carry = (weight_sum + weight_term.astype(jnp.bfloat16).astype(jnp.float32), conv_sum + grad_scale * d_conv, bias_sum + grad_scale * d_bias, rate_sum + grad_scale * d_rate, skip_sum + grad_scale * d_skip)
        return (carry, input_grad.astype(jnp.bfloat16))
    start_carry = (jnp.zeros((D, CH + HEADS), jnp.float32), jnp.zeros((KCONV, CH), jnp.float32), jnp.zeros((HEADS,), jnp.float32), jnp.zeros((HEADS,), jnp.float32), jnp.zeros((HEADS,), jnp.float32))
    final_carry, input_grads = lax.scan(per_sequence, start_carry, (layer_input, xbc_raw, dt_raw, grad_out))
    weight_sum, conv_sum, bias_sum, rate_sum, skip_sum = final_carry
    return (input_grads, weight_sum[:, :CH].astype(jnp.bfloat16), weight_sum[:, CH:].astype(jnp.bfloat16), conv_sum, bias_sum, rate_sum, skip_sum)
```

```python
import functools
import math

import jax
import jax.numpy as jnp
from jax import lax
from jax.experimental import pallas as pl
from jax.experimental.pallas import tpu as pltpu
from jax.sharding import PartitionSpec as P

HEAD_DIM = 64
STATE = 128
BLOCK = 128
HG = 8
HALO = 8
XW = HG * HEAD_DIM
GW = XW + 2 * STATE
F32 = jnp.float32
BF16 = jnp.bfloat16


def dot(a, b, ca, cb, precision=None):
    return lax.dot_general(
        a, b, (((ca,), (cb,)), ((), ())), preferred_element_type=F32, precision=precision
    )


def split_sum(indicator, z):
    hi = z.astype(BF16)
    lo = (z - hi.astype(F32)).astype(BF16)
    return dot(indicator, hi, 1, 1) + dot(indicator, lo, 1, 1)


def spread(columns, first):
    low = lax.broadcasted_iota(jnp.int32, (BLOCK, 2 * HEAD_DIM), 1) < HEAD_DIM
    parts = []
    for pair in range(HG // 2):
        at = first + 2 * pair
        left = jnp.broadcast_to(columns[:, at : at + 1], (BLOCK, 2 * HEAD_DIM))
        right = jnp.broadcast_to(columns[:, at + 1 : at + 2], (BLOCK, 2 * HEAD_DIM))
        parts.append(jnp.where(low, left, right))
    return jnp.concatenate(parts, axis=1)


def scan_kernel(
    raw_ref, gout_ref, dt_ref, taps_ref, head_ref, skip_ref,
    draw_ref, doff_ref, dconv_ref, dskip_ref, dhead_ref,
    rawpad, conv_s, act_s, cols_s, states, lam, tail,
):
    length = raw_ref.shape[0]
    blocks = length // BLOCK
    taps = taps_ref[...]
    kconv = taps.shape[0]
    bias = head_ref[:, 0:1]
    rate = head_ref[:, 1:2]
    rows = lax.broadcasted_iota(jnp.int32, (BLOCK, BLOCK), 0)
    lanes = lax.broadcasted_iota(jnp.int32, (BLOCK, BLOCK), 1)
    upto = (rows <= lanes).astype(F32)
    ahead = rows <= lanes
    hi_prec = lax.Precision.HIGHEST
    head_of = lax.broadcasted_iota(jnp.int32, (HG, XW), 1) // HEAD_DIM
    indicator = (head_of == lax.broadcasted_iota(jnp.int32, (HG, XW), 0)).astype(BF16)
    low = lax.broadcasted_iota(jnp.int32, (BLOCK, 2 * HEAD_DIM), 1) < HEAD_DIM

    def steps(start):
        pre = dt_ref[:, pl.ds(start, BLOCK)].astype(F32) + bias
        step = jnp.maximum(pre, 0.0) + jnp.log1p(jnp.exp(-jnp.abs(pre)))
        run = dot(-rate * step, upto, 1, 0, hi_prec)
        end = run[:, BLOCK - 1 : BLOCK]
        return pre, step, run, jnp.exp(end - run)

    rawpad[0:HALO, :] = jnp.zeros((HALO, GW), F32)
    states[0] = jnp.zeros((STATE, XW), F32)

    def forward(n, carry):
        start = pl.multiple_of(n * BLOCK, BLOCK)
        rawpad[pl.ds(pl.multiple_of(start + HALO, 8), BLOCK), :] = raw_ref[
            pl.ds(start, BLOCK), :
        ].astype(F32)
        window = rawpad[pl.ds(start, BLOCK + HALO), :]
        base = HALO - (kconv - 1)
        conv = taps[0:1] * window[base : base + BLOCK]
        for j in range(1, kconv):
            conv = conv + taps[j : j + 1] * window[base + j : base + j + BLOCK]
        conv_s[pl.ds(start, BLOCK), :] = conv
        act = (conv * jax.nn.sigmoid(conv)).astype(BF16)
        act_s[pl.ds(start, BLOCK), :] = act
        _, step, run, fall = steps(start)
        packed = jnp.concatenate(
            [run - jnp.log(step), fall * step, jnp.exp(run), jnp.zeros((BLOCK - 3 * HG, BLOCK), F32)],
            axis=0,
        )
        cols = packed.T
        cols_s[pl.ds(start, BLOCK), :] = cols
        weighted = (spread(cols, HG) * act[:, :XW].astype(F32)).astype(BF16)
        contrib = dot(act[:, XW : XW + STATE], weighted, 0, 0)
        factor = spread(cols, 2 * HG)[BLOCK - 1 : BLOCK]

        @pl.when(n < blocks - 1)
        def _():
            states[n + 1] = factor * states[n] + contrib

        return carry

    lax.fori_loop(0, blocks, forward, 0)

    lam[...] = jnp.zeros_like(lam)
    tail[...] = jnp.zeros_like(tail)
    dconv_ref[...] = jnp.zeros_like(dconv_ref)
    dskip_ref[...] = jnp.zeros_like(dskip_ref)
    dhead_ref[...] = jnp.zeros_like(dhead_ref)

    def backward(back, carry):
        n = blocks - 1 - back
        start = pl.multiple_of(n * BLOCK, BLOCK)
        act = act_s[pl.ds(start, BLOCK), :]
        x, b, c = act[:, :XW], act[:, XW : XW + STATE], act[:, XW + STATE :]
        g = gout_ref[pl.ds(start, BLOCK), :]
        xf, gf = x.astype(F32), g.astype(F32)
        cols = cols_s[pl.ds(start, BLOCK), :]
        pre, step, run, fall = steps(start)
        to_end = spread(cols, HG)
        grow = spread(cols, 2 * HG)
        factor = grow[BLOCK - 1 : BLOCK]
        entering = states[n]
        entering_b = entering.astype(BF16)
        lam_next = lam[...]
        lam_b = lam_next.astype(BF16)

        met = dot(c, entering_b, 1, 0)
        d_met = gf * grow
        d_met_b = d_met.astype(BF16)
        d_enter = dot(c, d_met_b, 0, 0)
        d_c = dot(d_met_b, entering_b, 1, 1)
        weighted = (to_end * xf).astype(BF16)
        d_weighted = dot(b, lam_b, 1, 0)
        d_b = dot(weighted, lam_b, 1, 1)
        lam[...] = factor * lam_next + d_enter
        d_factor = factor * jnp.sum(lam_next * entering, axis=0, keepdims=True)
        last = lax.broadcasted_iota(jnp.int32, (BLOCK, XW), 0) == BLOCK - 1
        ds = split_sum(indicator, d_met * met + jnp.where(last, d_factor, 0.0))
        d_to_end = split_sum(indicator, d_weighted * xf)

        scores = dot(b, c, 1, 1)
        d_scores = jnp.zeros((BLOCK, BLOCK), F32)
        by_key = jnp.zeros((BLOCK, BLOCK), F32)
        by_query = []
        d_x = []
        for pair in range(HG // 2):
            at = pair * 2 * HEAD_DIM
            x_pair = x[:, at : at + 2 * HEAD_DIM]
            g_pair = g[:, at : at + 2 * HEAD_DIM]
            zero = jnp.zeros_like(g_pair)
            mixes, kept = [], []
            for half in range(2):
                h = 2 * pair + half
                g_half = jnp.where(low, g_pair, zero) if half == 0 else jnp.where(low, zero, g_pair)
                d_mix = dot(x_pair, g_half, 1, 1)
                gap = run[h : h + 1] - cols[:, h : h + 1]
                reach = jnp.exp(jnp.where(ahead, gap, -1e30))
                mixes.append((scores * reach).astype(BF16))
                kept.append(g_half)
                d_part = d_mix * reach
                d_scores = d_scores + d_part
                pull = d_part * scores
                by_query.append(jnp.sum(pull, axis=0, keepdims=True))
                by_key = jnp.where(lanes == h, jnp.sum(pull, axis=1, keepdims=True), by_key)
            d_x.append(
                dot(jnp.concatenate(mixes, axis=1), jnp.concatenate(kept, axis=0), 1, 0)
            )
        d_scores_b = d_scores.astype(BF16)
        d_b = d_b + dot(d_scores_b, c, 1, 0)
        d_c = d_c + dot(d_scores_b, b, 0, 0)
        d_x = jnp.concatenate(d_x, axis=1) + to_end * d_weighted + skip_ref[...] * gf
        dskip_ref[...] += jnp.sum(gf * xf, axis=0, keepdims=True)

        key_sum = by_key.T[:HG]
        pulled = d_to_end * fall * step
        ds = ds + jnp.concatenate(by_query, axis=0) - key_sum - pulled
        lane8 = lax.broadcasted_iota(jnp.int32, (HG, BLOCK), 1)
        ds = ds + jnp.where(lane8 == BLOCK - 1, jnp.sum(pulled, axis=1, keepdims=True), 0.0)
        d_log = dot(ds, upto, 1, 1, hi_prec)
        d_step = key_sum / step + d_to_end * fall - rate * d_log
        d_off = d_step * jax.nn.sigmoid(pre)
        doff_ref[:, pl.ds(start, BLOCK)] = d_off.astype(BF16)
        totals = jnp.where(
            lane8 == 0,
            jnp.sum(d_off, axis=1, keepdims=True),
            jnp.where(lane8 == 1, -jnp.sum(d_log * step, axis=1, keepdims=True), 0.0),
        )
        dhead_ref[...] += totals

        conv = conv_s[pl.ds(start, BLOCK), :]
        sig = jax.nn.sigmoid(conv)
        d_act = jnp.concatenate([d_x, d_b, d_c], axis=1)
        d_conv = d_act * (sig * (1.0 + conv * (1.0 - sig)))
        onward = jnp.concatenate([d_conv, tail[...]], axis=0)
        tail[...] = d_conv[:HALO]
        window = rawpad[pl.ds(start, BLOCK + HALO), :]
        base = HALO - (kconv - 1)
        d_raw = jnp.zeros((BLOCK, GW), F32)
        for j in range(kconv):
            ahead_by = kconv - 1 - j
            d_raw = d_raw + taps[j : j + 1] * onward[ahead_by : ahead_by + BLOCK]
            dconv_ref[j : j + 1, :] += jnp.sum(
                d_conv * window[base + j : base + j + BLOCK], axis=0, keepdims=True
            )
        draw_ref[pl.ds(start, BLOCK), :] = d_raw.astype(BF16)
        return carry

    lax.fori_loop(0, blocks, backward, 0)


def scan_backward(tokens, offsets, conv_weight, head_rows, skip_wide, columns, interpret=False):
    length = tokens.shape[0]
    groups = columns // GW
    heads = groups * HG
    first = columns // XW
    kconv = conv_weight.shape[0]
    blocks = length // BLOCK
    return pl.pallas_call(
        scan_kernel,
        grid=(groups,),
        in_specs=[
            pl.BlockSpec((length, GW), lambda g: (0, g)),
            pl.BlockSpec((length, XW), lambda g: (0, first + g)),
            pl.BlockSpec((HG, length), lambda g: (g, 0)),
            pl.BlockSpec((kconv, GW), lambda g: (0, g)),
            pl.BlockSpec((HG, 2), lambda g: (g, 0)),
            pl.BlockSpec((1, XW), lambda g: (0, g)),
        ],
        out_specs=[
            pl.BlockSpec((length, GW), lambda g: (0, g)),
            pl.BlockSpec((HG, length), lambda g: (g, 0)),
            pl.BlockSpec((kconv, GW), lambda g: (0, g)),
            pl.BlockSpec((1, XW), lambda g: (0, g)),
            pl.BlockSpec((HG, BLOCK), lambda g: (g, 0)),
        ],
        out_shape=[
            jax.ShapeDtypeStruct((length, columns), BF16),
            jax.ShapeDtypeStruct((heads, length), BF16),
            jax.ShapeDtypeStruct((kconv, columns), F32),
            jax.ShapeDtypeStruct((1, groups * XW), F32),
            jax.ShapeDtypeStruct((heads, BLOCK), F32),
        ],
        scratch_shapes=[
            pltpu.VMEM((length + HALO, GW), F32),
            pltpu.VMEM((length, GW), F32),
            pltpu.VMEM((length, GW), BF16),
            pltpu.VMEM((length, BLOCK), F32),
            pltpu.VMEM((blocks, STATE, XW), F32),
            pltpu.VMEM((STATE, XW), F32),
            pltpu.VMEM((HALO, GW), F32),
        ],
        compiler_params=pltpu.CompilerParams(vmem_limit_bytes=48 * 1024 * 1024),
        cost_estimate=pl.CostEstimate(
            flops=length * columns * 2000, bytes_accessed=length * columns * 6, transcendentals=0
        ),
        interpret=interpret,
    )(tokens, tokens, offsets, conv_weight, head_rows, skip_wide)


def to_heads(x, parts):
    return x.reshape(x.shape[0], parts, x.shape[1] // parts).swapaxes(0, 1)


def sum_over(values, axis):
    size = lax.axis_size(axis)
    if size & (size - 1):
        return lax.psum(values, axis)
    hop = 1
    while hop < size:
        other = lax.ppermute(values, axis, [(i, i ^ hop) for i in range(size)])
        values = values + other
        hop *= 2
    return values


def local(
    layer_input, xbc_raw, dt_raw, grad_out, w_xbc, w_dt, conv_weight, dt_bias, decay_rate, skip_gain
):
    n_ctx = lax.axis_size("ctx")
    me = lax.axis_index("ctx")
    columns = w_xbc.shape[1]
    local_tokens = layer_input.shape[1]
    seq_len = n_ctx * local_tokens
    heads = dt_bias.shape[0]
    grad_scale = 1.0 / math.sqrt(lax.axis_size("fsdp") * seq_len)

    packed = jnp.concatenate([to_heads(xbc_raw[0], n_ctx), to_heads(grad_out[0], n_ctx)], axis=2)
    tokens = lax.all_to_all(packed, "ctx", split_axis=0, concat_axis=0, tiled=True)
    tokens = tokens.reshape(seq_len, packed.shape[2])
    offsets = lax.all_to_all(
        dt_raw[0].T.reshape(n_ctx, heads, local_tokens), "ctx", split_axis=0, concat_axis=0, tiled=True
    )
    offsets = offsets.swapaxes(0, 1).reshape(heads, seq_len)
    inputs = lax.all_gather(layer_input[0], "ctx", axis=0, tiled=True)
    weights = lax.all_gather(jnp.concatenate([w_xbc, w_dt], axis=1), "fsdp", axis=0, tiled=True)

    d_raw, d_off, d_conv, d_skip, d_head = scan_backward(
        tokens,
        offsets,
        conv_weight,
        jnp.stack([dt_bias, decay_rate], axis=1),
        jnp.repeat(skip_gain, HEAD_DIM)[None],
        columns,
    )
    grads = jnp.concatenate([d_raw, d_off.T], axis=1)
    running = lax.dot_general(
        inputs, grads, (((0,), (0,)), ((), ())), preferred_element_type=F32
    )
    running = (running * grad_scale).astype(BF16)
    grads, running = lax.optimization_barrier((grads, running))
    weight_grad = lax.psum_scatter(running, "fsdp", scatter_dimension=0, tiled=True)

    small = jnp.concatenate(
        [
            d_conv.reshape(-1),
            d_head[:, :2].T.reshape(-1),
            jnp.sum(d_skip.reshape(heads, HEAD_DIM), axis=1),
        ]
    )
    small = sum_over(small * grad_scale, "fsdp")
    taps = d_conv.size
    conv_grad = small[:taps].reshape(d_conv.shape)
    bias_grad, rate_grad, skip_grad = (
        small[taps + i * heads : taps + (i + 1) * heads] for i in range(3)
    )

    partial = lax.dot_general(
        grads, weights, (((1,), (1,)), ((), ())), preferred_element_type=F32
    ).astype(BF16)

    def rows_for(device):
        return lax.dynamic_slice_in_dim(partial, device * local_tokens, local_tokens, axis=0)

    total = rows_for(me).astype(F32)
    for k in range(1, n_ctx):
        got = lax.ppermute(
            rows_for(lax.rem(me + k, n_ctx)), "ctx", [(i, (i + k) % n_ctx) for i in range(n_ctx)]
        )
        total = total + got.astype(F32)
    input_grad = total.astype(BF16)[None]
    return (
        input_grad,
        weight_grad[:, :columns],
        weight_grad[:, columns:],
        conv_grad,
        bias_grad,
        rate_grad,
        skip_grad,
    )


def solution(mesh):
    return jax.shard_map(
        local,
        mesh=mesh,
        in_specs=(
            P("fsdp", "ctx", None),
            P("fsdp", "ctx", None),
            P("fsdp", "ctx", None),
            P("fsdp", "ctx", None),
            P("fsdp", "ctx"),
            P("fsdp", "ctx"),
            P(None, "ctx"),
            P("ctx"),
            P("ctx"),
            P("ctx"),
        ),
        out_specs=(
            P("fsdp", "ctx", None),
            P("fsdp", "ctx"),
            P("fsdp", "ctx"),
            P(None, "ctx"),
            P("ctx"),
            P("ctx"),
            P("ctx"),
        ),
        check_vma=False,
    )
```

```python
import math

import jax
import jax.numpy as jnp
from jax import lax
from jax.experimental import pallas as pl
from jax.experimental.pallas import tpu as pltpu
from jax.sharding import PartitionSpec as P


HEAD_DIM = 64
STATE = 128
BLOCK = 128
HG = 8
HALO = 8
XW = HG * HEAD_DIM
GW = XW + 2 * STATE
F32 = jnp.float32
BF16 = jnp.bfloat16


def dot(a, b, ca, cb, precision=None):
    return lax.dot_general(
        a, b, (((ca,), (cb,)), ((), ())), preferred_element_type=F32, precision=precision
    )


def split_sum(indicator, z):
    hi = z.astype(BF16)
    lo = (z - hi.astype(F32)).astype(BF16)
    return dot(indicator, hi, 1, 1) + dot(indicator, lo, 1, 1)


def spread(columns, first):
    low = lax.broadcasted_iota(jnp.int32, (BLOCK, 2 * HEAD_DIM), 1) < HEAD_DIM
    parts = []
    for pair in range(HG // 2):
        at = first + 2 * pair
        left = jnp.broadcast_to(columns[:, at : at + 1], (BLOCK, 2 * HEAD_DIM))
        right = jnp.broadcast_to(columns[:, at + 1 : at + 2], (BLOCK, 2 * HEAD_DIM))
        parts.append(jnp.where(low, left, right))
    return jnp.concatenate(parts, axis=1)


def scan_kernel(
    raw_ref, gout_ref, dt_ref, taps_ref, head_ref, skip_ref,
    draw_ref, doff_ref, dconv_ref, dskip_ref, dhead_ref,
    rawpad, conv_s, act_s, cols_s, states, lam, tail, dt_s,
):
    length = raw_ref.shape[0]
    blocks = length // BLOCK
    taps = taps_ref[...]
    first_head = pl.multiple_of(pl.program_id(0) * HG, HG)
    kconv = taps.shape[0]
    bias = head_ref[:, 0:1]
    rate = head_ref[:, 1:2]
    rows = lax.broadcasted_iota(jnp.int32, (BLOCK, BLOCK), 0)
    lanes = lax.broadcasted_iota(jnp.int32, (BLOCK, BLOCK), 1)
    upto = (rows <= lanes).astype(F32)
    ahead = rows <= lanes
    hi_prec = lax.Precision.HIGHEST
    head_of = lax.broadcasted_iota(jnp.int32, (HG, XW), 1) // HEAD_DIM
    indicator = (head_of == lax.broadcasted_iota(jnp.int32, (HG, XW), 0)).astype(BF16)
    low = lax.broadcasted_iota(jnp.int32, (BLOCK, 2 * HEAD_DIM), 1) < HEAD_DIM

    def steps(start):
        pre = dt_s[pl.ds(first_head, HG), pl.ds(start, BLOCK)] + bias
        step = jnp.maximum(pre, 0.0) + jnp.log1p(jnp.exp(-jnp.abs(pre)))
        run = dot(-rate * step, upto, 1, 0, hi_prec)
        end = run[:, BLOCK - 1 : BLOCK]
        return pre, step, run, jnp.exp(end - run)

    rawpad[0:HALO, :] = jnp.zeros((HALO, GW), F32)
    states[0] = jnp.zeros((STATE, XW), F32)

    def forward(n, carry):
        start = pl.multiple_of(n * BLOCK, BLOCK)
        rawpad[pl.ds(pl.multiple_of(start + HALO, 8), BLOCK), :] = raw_ref[
            pl.ds(start, BLOCK), :
        ].astype(F32)
        window = rawpad[pl.ds(start, BLOCK + HALO), :]
        base = HALO - (kconv - 1)
        conv = taps[0:1] * window[base : base + BLOCK]
        for j in range(1, kconv):
            conv = conv + taps[j : j + 1] * window[base + j : base + j + BLOCK]
        conv_s[pl.ds(start, BLOCK), :] = conv
        act = (conv * jax.nn.sigmoid(conv)).astype(BF16)
        act_s[pl.ds(start, BLOCK), :] = act
        dt_s[:, pl.ds(start, BLOCK)] = dt_ref[pl.ds(start, BLOCK), :].astype(F32).T
        _, step, run, fall = steps(start)
        packed = jnp.concatenate(
            [run - jnp.log(step), fall * step, jnp.exp(run), jnp.zeros((BLOCK - 3 * HG, BLOCK), F32)],
            axis=0,
        )
        cols = packed.T
        cols_s[pl.ds(start, BLOCK), :] = cols
        weighted = (spread(cols, HG) * act[:, :XW].astype(F32)).astype(BF16)
        contrib = dot(act[:, XW : XW + STATE], weighted, 0, 0)
        factor = spread(cols, 2 * HG)[BLOCK - 1 : BLOCK]

        @pl.when(n < blocks - 1)
        def _():
            states[n + 1] = factor * states[n] + contrib

        return carry

    lax.fori_loop(0, blocks, forward, 0)

    lam[...] = jnp.zeros_like(lam)
    tail[...] = jnp.zeros_like(tail)
    dconv_ref[...] = jnp.zeros_like(dconv_ref)
    dskip_ref[...] = jnp.zeros_like(dskip_ref)
    dhead_ref[...] = jnp.zeros_like(dhead_ref)

    def backward(back, carry):
        n = blocks - 1 - back
        start = pl.multiple_of(n * BLOCK, BLOCK)
        act = act_s[pl.ds(start, BLOCK), :]
        x, b, c = act[:, :XW], act[:, XW : XW + STATE], act[:, XW + STATE :]
        g = gout_ref[pl.ds(start, BLOCK), :]
        xf, gf = x.astype(F32), g.astype(F32)
        cols = cols_s[pl.ds(start, BLOCK), :]
        pre, step, run, fall = steps(start)
        to_end = spread(cols, HG)
        grow = spread(cols, 2 * HG)
        factor = grow[BLOCK - 1 : BLOCK]
        entering = states[n]
        entering_b = entering.astype(BF16)
        lam_next = lam[...]
        lam_b = lam_next.astype(BF16)

        met = dot(c, entering_b, 1, 0)
        d_met = gf * grow
        d_met_b = d_met.astype(BF16)
        d_enter = dot(c, d_met_b, 0, 0)
        d_c = dot(d_met_b, entering_b, 1, 1)
        weighted = (to_end * xf).astype(BF16)
        d_weighted = dot(b, lam_b, 1, 0)
        d_b = dot(weighted, lam_b, 1, 1)
        lam[...] = factor * lam_next + d_enter
        d_factor = factor * jnp.sum(lam_next * entering, axis=0, keepdims=True)
        last = lax.broadcasted_iota(jnp.int32, (BLOCK, XW), 0) == BLOCK - 1
        ds = split_sum(indicator, d_met * met + jnp.where(last, d_factor, 0.0))
        d_to_end = split_sum(indicator, d_weighted * xf)

        scores = dot(b, c, 1, 1)
        d_scores = jnp.zeros((BLOCK, BLOCK), F32)
        by_key = jnp.zeros((BLOCK, BLOCK), F32)
        by_query = []
        d_x = []
        for pair in range(HG // 2):
            at = pair * 2 * HEAD_DIM
            x_pair = x[:, at : at + 2 * HEAD_DIM]
            g_pair = g[:, at : at + 2 * HEAD_DIM]
            zero = jnp.zeros_like(g_pair)
            mixes, kept = [], []
            for half in range(2):
                h = 2 * pair + half
                g_half = jnp.where(low, g_pair, zero) if half == 0 else jnp.where(low, zero, g_pair)
                d_mix = dot(x_pair, g_half, 1, 1)
                gap = run[h : h + 1] - cols[:, h : h + 1]
                reach = jnp.exp(jnp.where(ahead, gap, -1e30))
                mixes.append((scores * reach).astype(BF16))
                kept.append(g_half)
                d_part = d_mix * reach
                d_scores = d_scores + d_part
                pull = d_part * scores
                by_query.append(jnp.sum(pull, axis=0, keepdims=True))
                by_key = jnp.where(lanes == h, jnp.sum(pull, axis=1, keepdims=True), by_key)
            d_x.append(
                dot(jnp.concatenate(mixes, axis=1), jnp.concatenate(kept, axis=0), 1, 0)
            )
        d_scores_b = d_scores.astype(BF16)
        d_b = d_b + dot(d_scores_b, c, 1, 0)
        d_c = d_c + dot(d_scores_b, b, 0, 0)
        d_x = jnp.concatenate(d_x, axis=1) + to_end * d_weighted + skip_ref[...] * gf
        dskip_ref[...] += jnp.sum(gf * xf, axis=0, keepdims=True)

        key_sum = by_key.T[:HG]
        pulled = d_to_end * fall * step
        ds = ds + jnp.concatenate(by_query, axis=0) - key_sum - pulled
        lane8 = lax.broadcasted_iota(jnp.int32, (HG, BLOCK), 1)
        ds = ds + jnp.where(lane8 == BLOCK - 1, jnp.sum(pulled, axis=1, keepdims=True), 0.0)
        d_log = dot(ds, upto, 1, 1, hi_prec)
        d_step = key_sum / step + d_to_end * fall - rate * d_log
        d_off = d_step * jax.nn.sigmoid(pre)
        doff_ref[:, pl.ds(start, BLOCK)] = d_off.astype(BF16)
        totals = jnp.where(
            lane8 == 0,
            jnp.sum(d_off, axis=1, keepdims=True),
            jnp.where(lane8 == 1, -jnp.sum(d_log * step, axis=1, keepdims=True), 0.0),
        )
        dhead_ref[...] += totals

        conv = conv_s[pl.ds(start, BLOCK), :]
        sig = jax.nn.sigmoid(conv)
        d_act = jnp.concatenate([d_x, d_b, d_c], axis=1)
        d_conv = d_act * (sig * (1.0 + conv * (1.0 - sig)))
        onward = jnp.concatenate([d_conv, tail[...]], axis=0)
        tail[...] = d_conv[:HALO]
        window = rawpad[pl.ds(start, BLOCK + HALO), :]
        base = HALO - (kconv - 1)
        d_raw = jnp.zeros((BLOCK, GW), F32)
        for j in range(kconv):
            ahead_by = kconv - 1 - j
            d_raw = d_raw + taps[j : j + 1] * onward[ahead_by : ahead_by + BLOCK]
            dconv_ref[j : j + 1, :] += jnp.sum(
                d_conv * window[base + j : base + j + BLOCK], axis=0, keepdims=True
            )
        draw_ref[pl.ds(start, BLOCK), :] = d_raw.astype(BF16)
        return carry

    lax.fori_loop(0, blocks, backward, 0)


def scan_backward(tokens, conv_weight, head_rows, skip_wide, columns, interpret=False):
    length = tokens.shape[0]
    groups = columns // GW
    heads = groups * HG
    first = columns // XW
    dt_wide = tokens.shape[1] - columns - groups * XW
    dt_at = (columns + groups * XW) // dt_wide
    kconv = conv_weight.shape[0]
    blocks = length // BLOCK
    return pl.pallas_call(
        scan_kernel,
        grid=(groups,),
        in_specs=[
            pl.BlockSpec((length, GW), lambda g: (0, g)),
            pl.BlockSpec((length, XW), lambda g: (0, first + g)),
            pl.BlockSpec((length, dt_wide), lambda g: (0, dt_at)),
            pl.BlockSpec((kconv, GW), lambda g: (0, g)),
            pl.BlockSpec((HG, 2), lambda g: (g, 0)),
            pl.BlockSpec((1, XW), lambda g: (0, g)),
        ],
        out_specs=[
            pl.BlockSpec((length, GW), lambda g: (0, g)),
            pl.BlockSpec((HG, length), lambda g: (g, 0)),
            pl.BlockSpec((kconv, GW), lambda g: (0, g)),
            pl.BlockSpec((1, XW), lambda g: (0, g)),
            pl.BlockSpec((HG, BLOCK), lambda g: (g, 0)),
        ],
        out_shape=[
            jax.ShapeDtypeStruct((length, columns), BF16),
            jax.ShapeDtypeStruct((heads, length), BF16),
            jax.ShapeDtypeStruct((kconv, columns), F32),
            jax.ShapeDtypeStruct((1, groups * XW), F32),
            jax.ShapeDtypeStruct((heads, BLOCK), F32),
        ],
        scratch_shapes=[
            pltpu.VMEM((length + HALO, GW), F32),
            pltpu.VMEM((length, GW), F32),
            pltpu.VMEM((length, GW), BF16),
            pltpu.VMEM((length, BLOCK), F32),
            pltpu.VMEM((blocks, STATE, XW), F32),
            pltpu.VMEM((STATE, XW), F32),
            pltpu.VMEM((HALO, GW), F32),
            pltpu.VMEM((dt_wide, length), F32),
        ],
        compiler_params=pltpu.CompilerParams(vmem_limit_bytes=48 * 1024 * 1024),
        cost_estimate=pl.CostEstimate(
            flops=length * columns * 30000, bytes_accessed=length * columns * 6, transcendentals=0
        ),
        interpret=interpret,
    )(tokens, tokens, tokens, conv_weight, head_rows, skip_wide)


def to_heads(x, parts):
    return x.reshape(x.shape[0], parts, x.shape[1] // parts).swapaxes(0, 1)


def sum_over(values, axis):
    size = lax.axis_size(axis)
    if size & (size - 1):
        return lax.psum(values, axis)
    hop = 1
    while hop < size:
        other = lax.ppermute(values, axis, [(i, i ^ hop) for i in range(size)])
        values = values + other
        hop *= 2
    return values


def ring_blocks(block, axis):
    size = lax.axis_size(axis)
    onward = [(i, (i + 2) % size) for i in range(size)]
    blocks = [block]
    for _ in range(1, size // 2):
        blocks.append(lax.ppermute(blocks[-1], axis, onward))
    return blocks


def with_other_core(blocks, axis):
    across = [(i, i ^ 1) for i in range(lax.axis_size(axis))]
    return [b for block in blocks for b in (block, lax.ppermute(block, axis, across))]


def in_order(x, axis):
    size = lax.axis_size(axis)
    width = x.shape[1] // size
    me = lax.axis_index(axis)
    parts = []
    for owner in range(size):
        back = lax.rem(me // 2 - owner // 2 + size // 2, size // 2)
        place = 2 * back + (me + owner) % 2
        parts.append(lax.dynamic_slice_in_dim(x, place * width, width, axis=1))
    return jnp.concatenate(parts, axis=1)


def mixer_backward(
    layer_input, xbc_raw, dt_raw, grad_out, w_xbc, w_dt, conv_weight, dt_bias, decay_rate, skip_gain
):
    n_ctx = lax.axis_size("ctx")
    me = lax.axis_index("ctx")
    columns = w_xbc.shape[1]
    local_tokens = layer_input.shape[1]
    seq_len = n_ctx * local_tokens
    heads = dt_bias.shape[0]
    grad_scale = 1.0 / math.sqrt(lax.axis_size("fsdp") * seq_len)

    weight_cat = jnp.concatenate([w_xbc, w_dt], axis=1)
    xbc_raw, weight_cat = lax.optimization_barrier((xbc_raw, weight_cat))
    weights = ring_blocks(weight_cat, "fsdp")
    padding = -heads % 128
    packed = jnp.concatenate(
        [
            to_heads(xbc_raw[0], n_ctx),
            to_heads(grad_out[0], n_ctx),
            jnp.pad(to_heads(dt_raw[0], n_ctx), ((0, 0), (0, 0), (0, padding))),
        ],
        axis=2,
    )
    tokens = lax.all_to_all(packed, "ctx", split_axis=0, concat_axis=0, tiled=True)
    tokens = tokens.reshape(seq_len, packed.shape[2])
    inputs = lax.all_gather(layer_input[0], "ctx", axis=0, tiled=True)

    tokens, weights[1] = lax.optimization_barrier((tokens, weights[1]))
    d_raw, d_off, d_conv, d_skip, d_head = scan_backward(
        tokens,
        conv_weight,
        jnp.stack([dt_bias, decay_rate], axis=1),
        jnp.repeat(skip_gain, HEAD_DIM)[None],
        columns,
    )
    grads = jnp.concatenate([d_raw, d_off.T], axis=1)
    running = lax.dot_general(inputs, grads, (((0,), (0,)), ((), ())), preferred_element_type=F32)
    running = (running * grad_scale).astype(BF16)
    grads, running = lax.optimization_barrier((grads, running))
    weight_grad = lax.psum_scatter(running, "fsdp", scatter_dimension=0, tiled=True)

    small = jnp.concatenate(
        [
            d_conv.reshape(-1),
            d_head[:, :2].T.reshape(-1),
            jnp.sum(d_skip.reshape(heads, HEAD_DIM), axis=1),
        ]
    )
    small = sum_over(small * grad_scale, "fsdp")
    taps = d_conv.size
    conv_grad = small[:taps].reshape(d_conv.shape)
    bias_grad, rate_grad, skip_grad = (
        small[taps + i * heads : taps + (i + 1) * heads] for i in range(3)
    )

    partial = jnp.concatenate(
        [
            lax.dot_general(
                grads, block, (((1,), (1,)), ((), ())), preferred_element_type=F32
            ).astype(BF16)
            for block in with_other_core(weights, "fsdp")
        ],
        axis=1,
    )

    def rows_for(device):
        return lax.dynamic_slice_in_dim(partial, device * local_tokens, local_tokens, axis=0)

    total = rows_for(me).astype(F32)
    for k in range(1, n_ctx):
        got = lax.ppermute(
            rows_for(lax.rem(me + k, n_ctx)), "ctx", [(i, (i + k) % n_ctx) for i in range(n_ctx)]
        )
        total = total + got.astype(F32)
    input_grad = in_order(total.astype(BF16), "fsdp")[None]
    return (
        input_grad,
        weight_grad[:, :columns],
        weight_grad[:, columns:],
        conv_grad,
        bias_grad,
        rate_grad,
        skip_grad,
    )


def solution(mesh):
    return jax.shard_map(
        mixer_backward,
        mesh=mesh,
        in_specs=(
            P("fsdp", "ctx", None),
            P("fsdp", "ctx", None),
            P("fsdp", "ctx", None),
            P("fsdp", "ctx", None),
            P("fsdp", "ctx"),
            P("fsdp", "ctx"),
            P(None, "ctx"),
            P("ctx"),
            P("ctx"),
            P("ctx"),
        ),
        out_specs=(
            P("fsdp", "ctx", None),
            P("fsdp", "ctx"),
            P("fsdp", "ctx"),
            P(None, "ctx"),
            P("ctx"),
            P("ctx"),
            P("ctx"),
        ),
        check_vma=False,
    )
```
